32 devices in a mesh: grp: 4 (over y, core), dev: 8 (over z, x).
Axes of the slice: x: 2, y: 2, z: 4, core: 2. Of those that a mesh axis runs over, the one named last changes fastest.
Arguments:
- tokens: bfloat16 [4096, 2048], P(('grp', 'dev')), may hold values from -6 to 6
- cotangent: bfloat16 [4096, 2048], P(('grp', 'dev')), may hold values from -1.5 to 1.5
- route_weight: float32 [4096, 2], P(('grp', 'dev')), may hold values from 0.1 to 1
- slot_expert: int32 [32], replicated, may hold values from 0 to 15, as said below
- targets: int32 [4096, 2], P(('grp', 'dev')), may hold values from 0 to 31, as said below
- proj_in: float32 [16, 2048, 2048], P('grp', 'dev'), may hold values from -0.125 to 0.125
- first_in: float32 [16, 2048, 2048], P('grp', 'dev'), may hold values from -6 to 6
- second_in: float32 [16, 2048, 2048], P('grp', 'dev'), may hold values from 0.01 to 1
- proj_out: float32 [16, 1024, 2048], P('grp', 'dev'), may hold values from -0.1875 to 0.1875
- first_out: float32 [16, 1024, 2048], P('grp', 'dev'), may hold values from -6 to 6
- second_out: float32 [16, 1024, 2048], P('grp', 'dev'), may hold values from 0.01 to 1
Outputs:
- mixed: bfloat16 [4096, 2048], P(('grp', 'dev'))
- token_grad: bfloat16 [4096, 2048], P(('grp', 'dev'))
- mix_grad: float32 [4096, 2], P(('grp', 'dev'))
- trained_in: float32 [16, 2048, 2048], P('grp', 'dev')
- mean_in: float32 [16, 2048, 2048], P('grp', 'dev')
- square_in: float32 [16, 2048, 2048], P('grp', 'dev')
- trained_out: float32 [16, 1024, 2048], P('grp', 'dev')
- mean_out: float32 [16, 1024, 2048], P('grp', 'dev')
- square_out: float32 [16, 1024, 2048], P('grp', 'dev')
The draws below stay inside these ranges and needn't reach their ends.
Inputs may be any that keep to these rules, and one draw needn't show every extreme that they name: `slot_expert`: entry s is the expert held by slot s, the device s in grp+dev order; each of the 16 experts is held by at least one slot. `targets`: entry [t, k] is the slot that serves the k-th expert of token t; the two slots of a token hold different experts.
All inputs are finite; a program needn't handle non-finite values.
Results may differ from the reference program's by a relative error of at most 0.015.
The reference program's roundings to bfloat16 on the way count: a program that leaves them out, or rounds other values in their place, can miss the bound.
Values may be sent and summed in bfloat16 or wider, within the bound.
A program may use at most 192 MiB of HBM per device.

```python
import math
import jax
import jax.numpy as jnp
from jax import lax

D = 2048
FF = 1024
E = 16
TOK_DEV = 128
SLOTS = 32
TOKENS = 4096
CAP = 12
N_GRP = 4
N_DEV = 8


def route_plan(key):
    folded = jax.random.fold_in(key, 4243)
    subkeys = jax.random.split(folded, 6)
    shuffle = jax.random.permutation(subkeys[0], E)
    first_pick = jax.random.randint(subkeys[1], (SLOTS - E,), 0, E)
    second_pick = jax.random.randint(subkeys[2], (SLOTS - E,), 0, E)
    extras = shuffle[jnp.minimum(first_pick, second_pick)].astype(jnp.int32)
    filled = jnp.concatenate([jnp.arange(E, dtype=jnp.int32), extras])
    reorder = jax.random.permutation(subkeys[3], SLOTS)
    experts = filled[reorder].astype(jnp.int32)
    first_slot = jax.random.randint(subkeys[4], (TOKENS,), 0, SLOTS).astype(jnp.int32)
    first_expert = experts[first_slot]
    differ = (experts[None, :] != first_expert[:, None]).astype(jnp.int32)
    others = jnp.sum(differ, axis=1)
    chosen = jax.random.randint(subkeys[5], (TOKENS,), 0, others).astype(jnp.int32)
    running = jnp.cumsum(differ, axis=1)
    second_slot = jnp.sum((running <= chosen[:, None]).astype(jnp.int32), axis=1)
    return (experts, jnp.stack([first_slot, second_slot], axis=1).astype(jnp.int32))


def draw_slot_expert(key, part):
    return route_plan(key)[0]


def draw_targets(key, part):
    return route_plan(key)[1]


def level_of(stream_key, extent, cuts, low, high):
    gain = 1.0
    for dim, parts in cuts:
        heights = jax.random.uniform(jax.random.fold_in(jax.random.fold_in(stream_key, 6), dim), (parts,), jnp.float32, low / len(cuts), high / len(cuts))
        gain = gain * jnp.repeat(jnp.exp(heights), extent[dim] // parts).reshape((-1,) + (1,) * (len(extent) - 1 - dim))
    return gain


def bell_draw(rng, shape, scale, limit, cuts=(), kind=jnp.bfloat16):
    loudness = level_of(rng, shape, cuts, -0.22, 0.18) if cuts else 1.0
    drawn = jax.random.normal(rng, shape, jnp.float32) * scale * loudness
    return jnp.minimum(jnp.maximum(drawn, -limit), limit).astype(kind)


def setup_inputs(seed: int = 0) -> dict:
    splits = jax.random.split(jax.random.key(seed), 12)
    return {
        "tokens": bell_draw(splits[0], (TOKENS, D), 1.0, 6.0, ((0, 32),)),
        "cotangent": bell_draw(splits[1], (TOKENS, D), 0.25, 1.5, ((0, 32),)),
        "route_weight": jnp.clip(0.1 + 0.9 * jax.random.uniform(splits[2], (TOKENS, 2), jnp.float32) ** level_of(splits[2], (TOKENS, 2), ((0, 32),), -0.2, 0.2), 0.1, 1.0),
        "slot_expert": draw_slot_expert(jax.random.fold_in(splits[11], 71), 0),
        "targets": draw_targets(jax.random.fold_in(splits[11], 71), 0),
        "proj_in": bell_draw(splits[5], (E, D, 2 * FF), D ** -0.5, 0.125, ((0, 4), (1, 8)), jnp.float32),
        "first_in": bell_draw(splits[6], (E, D, 2 * FF), 1.0, 6.0, ((0, 4), (1, 8)), jnp.float32),
        "second_in": jnp.clip(jnp.exp(math.log(1.0) - 4.6051702 * jax.random.uniform(splits[7], (E, D, 2 * FF), jnp.float32) ** level_of(splits[7], (E, D, 2 * FF), ((0, 4), (1, 8)), -0.2, 0.2)), 0.01, 1.0),
        "proj_out": bell_draw(splits[8], (E, FF, D), FF ** -0.5, 0.1875, ((0, 4), (1, 8)), jnp.float32),
        "first_out": bell_draw(splits[9], (E, FF, D), 1.0, 6.0, ((0, 4), (1, 8)), jnp.float32),
        "second_out": jnp.clip(jnp.exp(math.log(1.0) - 4.6051702 * jax.random.uniform(splits[10], (E, FF, D), jnp.float32) ** level_of(splits[10], (E, FF, D), ((0, 4), (1, 8)), -0.2, 0.2)), 0.01, 1.0),
    }


beta_first = 0.9
beta_second = 0.95
learn_rate = 0.01
decay_rate = 0.1
adam_eps = 1e-08
bias_first = 1.0 - 0.9 ** 10
bias_second = 1.0 - 0.95 ** 10

def silu_parts(values):
    logistic = jax.nn.sigmoid(values)
    return (values * logistic, logistic * (1.0 + values * (1.0 - logistic)))

def slot_pass(rows_x, rows_dy, weight_up, weight_down):
    gate_up = jnp.dot(rows_x, weight_up, preferred_element_type=jnp.float32)
    gating = gate_up[:, :FF]
    upward = gate_up[:, FF:]
    active, derivative = silu_parts(gating)
    hidden = (active * upward).astype(jnp.bfloat16)
    result = jnp.dot(hidden, weight_down, preferred_element_type=jnp.float32).astype(jnp.bfloat16)
    dhidden = lax.dot_general(rows_dy, weight_down, (((1,), (1,)), ((), ())), preferred_element_type=jnp.float32)
    grad_gateup = jnp.concatenate([dhidden * upward * derivative, dhidden * active], axis=1).astype(jnp.bfloat16)
    rows_dx = lax.dot_general(grad_gateup, weight_up, (((1,), (1,)), ((), ())), preferred_element_type=jnp.float32).astype(jnp.bfloat16)
    grad_up = lax.dot_general(rows_x, grad_gateup, (((0,), (0,)), ((), ())), preferred_element_type=jnp.float32).astype(jnp.bfloat16)
    grad_down = lax.dot_general(hidden, rows_dy, (((0,), (0,)), ((), ())), preferred_element_type=jnp.float32).astype(jnp.bfloat16)
    return (result, rows_dx, grad_up, grad_down)

def adam_step(weight, moment, square, gradient):
    new_moment = beta_first * moment + (1.0 - beta_first) * gradient
    new_square = beta_second * square + (1.0 - beta_second) * gradient * gradient
    update = new_moment / bias_first / (jnp.sqrt(new_square / bias_second) + adam_eps) + decay_rate * weight
    return (weight - learn_rate * update, new_moment, new_square)

def reference(tokens, cotangent, route_weight, slot_expert, targets, proj_in, first_in, second_in, proj_out, first_out, second_out):
    assigns = 2 * TOK_DEV
    buffer_rows = SLOTS * CAP
    per_source = targets.reshape(SLOTS, assigns)
    slot_ids = jnp.arange(SLOTS, dtype=jnp.int32)
    onehot = (per_source[:, :, None] == slot_ids[None, None, :]).astype(jnp.int32)
    earlier = jnp.cumsum(onehot, axis=1) - onehot
    position = lax.optimization_barrier(jnp.sum(earlier * onehot, axis=2)).astype(jnp.int32)
    within = position < CAP
    landing = per_source * buffer_rows + slot_ids[:, None] * CAP + position
    landing = jnp.where(within, landing, SLOTS * buffer_rows).astype(jnp.int32)
    assign_ids = jnp.arange(SLOTS * assigns, dtype=jnp.int32)
    row_table = jnp.full((SLOTS * buffer_rows,), -1, jnp.int32).at[landing.reshape(-1)].set(assign_ids, mode='drop')
    row_table = row_table.reshape(SLOTS, buffer_rows)
    flat_weight = route_weight.reshape(-1)
    scaled = (flat_weight[:, None] * jnp.repeat(cotangent, 2, axis=0).astype(jnp.float32)).astype(jnp.bfloat16)

    def serve_slot(carried, slot_id):
        acc_up, acc_down, out_all, dx_all = carried
        entries = row_table[slot_id]
        filled = entries >= 0
        safe_ids = jnp.where(filled, entries, 0).astype(jnp.int32)
        rows_x = jnp.where(filled[:, None], tokens[safe_ids // 2], jnp.zeros((), tokens.dtype))
        rows_dy = jnp.where(filled[:, None], scaled[safe_ids], jnp.zeros((), scaled.dtype))
        expert = slot_expert[slot_id]
        weight_up = lax.dynamic_index_in_dim(proj_in, expert, 0, keepdims=False).astype(jnp.bfloat16)
        weight_down = lax.dynamic_index_in_dim(proj_out, expert, 0, keepdims=False).astype(jnp.bfloat16)
        result, rows_dx, grad_up, grad_down = slot_pass(rows_x, rows_dy, weight_up, weight_down)
        acc_up = acc_up.at[expert].add(grad_up.astype(jnp.float32))
        acc_down = acc_down.at[expert].add(grad_down.astype(jnp.float32))
        landing_row = jnp.where(filled, entries, 2 * TOKENS).astype(jnp.int32)
        out_all = out_all.at[landing_row].set(result, mode='drop')
        dx_all = dx_all.at[landing_row].set(rows_dx, mode='drop')
        return ((acc_up, acc_down, out_all, dx_all), None)
    total_up = jnp.zeros((E, D, 2 * FF), jnp.float32)
    total_down = jnp.zeros((E, FF, D), jnp.float32)
    out_all = jnp.zeros((2 * TOKENS, D), jnp.bfloat16)
    dx_all = jnp.zeros((2 * TOKENS, D), jnp.bfloat16)
    for group_id in range(N_GRP):
        start_up = jnp.zeros((E, D, 2 * FF), jnp.float32)
        start_down = jnp.zeros((E, FF, D), jnp.float32)
        slot_range = jnp.arange(group_id * N_DEV, (group_id + 1) * N_DEV, dtype=jnp.int32)
        finished, unused = lax.scan(serve_slot, (start_up, start_down, out_all, dx_all), slot_range)
        acc_up, acc_down, out_all, dx_all = finished
        total_up = total_up + lax.optimization_barrier(acc_up.astype(jnp.bfloat16)).astype(jnp.float32)
        total_down = total_down + lax.optimization_barrier(acc_down.astype(jnp.bfloat16)).astype(jnp.float32)
    out_float = out_all.reshape(TOKENS, 2, D).astype(jnp.float32)
    dx_pairs = dx_all.reshape(TOKENS, 2, D).astype(jnp.float32)
    mixed = (route_weight[:, 0:1] * out_float[:, 0] + route_weight[:, 1:2] * out_float[:, 1]).astype(jnp.bfloat16)
    token_grad = (dx_pairs[:, 0] + dx_pairs[:, 1]).astype(jnp.bfloat16)
    mix_grad = lax.optimization_barrier(jnp.sum(cotangent.astype(jnp.float32)[:, None, :] * out_float, axis=2))
    trained_in, mean_in, square_in = adam_step(proj_in, first_in, second_in, total_up)
    trained_out, mean_out, square_out = adam_step(proj_out, first_out, second_out, total_down)
    return (mixed, token_grad, mix_grad, trained_in, mean_in, square_in, trained_out, mean_out, square_out)
```

```python
import jax
import jax.numpy as jnp
from jax import lax
from jax.experimental import pallas as pl
from jax.experimental.pallas import tpu as pltpu
from jax.sharding import PartitionSpec as P

D = 2048
FF = 1024
E = 16


beta_first = 0.9
beta_second = 0.95
learn_rate = 0.01
decay_rate = 0.1
adam_eps = 1e-08
bias_first = 1.0 - 0.9**10
bias_second = 1.0 - 0.95**10


def silu_parts(values):
    logistic = jax.nn.sigmoid(values)
    return (values * logistic, logistic * (1.0 + values * (1.0 - logistic)))


def slot_pass(rows_x, rows_dy, weight_up, weight_down):
    gate_up = jnp.dot(rows_x, weight_up, preferred_element_type=jnp.float32)
    gating = gate_up[:, :FF]
    upward = gate_up[:, FF:]
    active, derivative = silu_parts(gating)
    hidden = (active * upward).astype(jnp.bfloat16)
    result = jnp.dot(hidden, weight_down, preferred_element_type=jnp.float32).astype(jnp.bfloat16)
    dhidden = lax.dot_general(
        rows_dy, weight_down, (((1,), (1,)), ((), ())), preferred_element_type=jnp.float32
    )
    grad_gateup = jnp.concatenate([dhidden * upward * derivative, dhidden * active], axis=1).astype(
        jnp.bfloat16
    )
    rows_dx = lax.dot_general(
        grad_gateup, weight_up, (((1,), (1,)), ((), ())), preferred_element_type=jnp.float32
    ).astype(jnp.bfloat16)
    grad_up = lax.dot_general(
        rows_x, grad_gateup, (((0,), (0,)), ((), ())), preferred_element_type=jnp.float32
    ).astype(jnp.bfloat16)
    grad_down = lax.dot_general(
        hidden, rows_dy, (((0,), (0,)), ((), ())), preferred_element_type=jnp.float32
    ).astype(jnp.bfloat16)
    return (result, rows_dx, grad_up, grad_down)


def adam_step(weight, moment, square, gradient):
    new_moment = beta_first * moment + (1.0 - beta_first) * gradient
    new_square = beta_second * square + (1.0 - beta_second) * gradient * gradient
    update = (
        new_moment / bias_first / (jnp.sqrt(new_square / bias_second) + adam_eps)
        + decay_rate * weight
    )
    return (weight - learn_rate * update, new_moment, new_square)


def after(value, *earlier):
    return lax.optimization_barrier((value,) + earlier)[0]


def expert_sums(experts, rows):
    members, depth, width = rows.shape
    tile = 16

    def kernel(expert_ref, rows_ref, out_ref, acc_ref):
        acc_ref[...] = jnp.zeros_like(acc_ref)

        def add(d, carry):
            e = expert_ref[d]
            acc_ref[e] = acc_ref[e] + rows_ref[d].astype(jnp.float32)
            return carry

        lax.fori_loop(0, members, add, 0)
        out_ref[...] = acc_ref[...].astype(out_ref.dtype)

    return pl.pallas_call(
        kernel,
        grid_spec=pltpu.PrefetchScalarGridSpec(
            num_scalar_prefetch=1,
            grid=(depth // tile,),
            in_specs=[pl.BlockSpec((members, tile, width), lambda i, e: (0, i, 0))],
            out_specs=pl.BlockSpec((E, tile, width), lambda i, e: (0, i, 0)),
            scratch_shapes=[pltpu.VMEM((E, tile, width), jnp.float32)],
        ),
        out_shape=jax.ShapeDtypeStruct((E, depth, width), jnp.bfloat16),
        compiler_params=pltpu.CompilerParams(vmem_limit_bytes=24 * 1024 * 1024),
        cost_estimate=pl.CostEstimate(
            flops=members * depth * width,
            bytes_accessed=2 * (members + E) * depth * width,
            transcendentals=0,
        ),
    )(experts, rows)


def pick_experts(stack, experts):
    return jnp.take(stack, experts, axis=0, mode="clip")


def exchange(payload, axes):
    return lax.all_to_all(payload, axes, split_axis=0, concat_axis=0, tiled=True)


def on_device(
    tokens,
    cotangent,
    route_weight,
    slot_expert,
    targets,
    proj_in,
    first_in,
    second_in,
    proj_out,
    first_out,
    second_out,
):
    groups = lax.axis_size("grp")
    members = lax.axis_size("dev")
    slot_count = groups * members
    everyone = ("grp", "dev")
    tok_count = tokens.shape[0]
    capacity = 3 * tok_count // slot_count
    pair = 2 * capacity
    pair_rows = slot_count * pair

    my_group = lax.axis_index("grp")
    group_expert = lax.dynamic_slice_in_dim(slot_expert, my_group * members, members)
    group_expert = jnp.clip(group_expert, 0, E - 1)
    low_out = proj_out.astype(jnp.bfloat16)
    all_down = lax.all_gather(low_out, "grp", axis=0, tiled=True)
    low_in = proj_in.astype(jnp.bfloat16)
    all_up = lax.all_gather(low_in, "grp", axis=0, tiled=True)

    flat_target = targets.reshape(-1)
    onehot = (flat_target[:, None] == jnp.arange(slot_count, dtype=jnp.int32)[None, :]).astype(
        jnp.int32
    )
    earlier = jnp.cumsum(onehot, axis=0) - onehot
    position = jnp.sum(earlier * onehot, axis=1)
    within = position < capacity
    row = jnp.where(within, flat_target * pair + position, -pair_rows).reshape(tok_count, 2)
    row_x = [row[:, 0], row[:, 1]]
    row_dy = [row[:, 0] + capacity, row[:, 1] + capacity]
    places = jnp.arange(pair_rows, dtype=jnp.int32)

    hit_x = (places[:, None] == row_x[0][None, :]) | (places[:, None] == row_x[1][None, :])
    hit_0 = places[:, None] == row_dy[0][None, :]
    hit_1 = places[:, None] == row_dy[1][None, :]
    picker = jnp.concatenate([hit_x, hit_0, hit_1], axis=1).astype(jnp.bfloat16)
    cot_float = cotangent.astype(jnp.float32)
    scaled = [(route_weight[:, k : k + 1] * cot_float).astype(jnp.bfloat16) for k in (0, 1)]
    source = jnp.concatenate([tokens] + scaled, axis=0)
    send = jnp.dot(picker, source, preferred_element_type=jnp.float32).astype(jnp.bfloat16)
    slot_both = exchange(send.reshape(slot_count, pair, D), everyone)

    got_down = exchange(after(pick_experts(all_down, group_expert), slot_both), "dev")
    got_up = exchange(after(pick_experts(all_up, group_expert), got_down), "dev")
    slot_x = slot_both[:, :capacity].reshape(slot_count * capacity, D)
    slot_dy = slot_both[:, capacity:].reshape(slot_count * capacity, D)
    slot_up = got_up.reshape(D, 2 * FF)
    slot_down = got_down.reshape(FF, D)
    result, rows_dx, grad_up, grad_down = slot_pass(slot_x, slot_dy, slot_up, slot_down)

    rows_up = exchange(grad_up.reshape(members, D // members, 2 * FF), "dev")
    part_up = expert_sums(group_expert, rows_up)
    back = jnp.concatenate(
        [result.reshape(slot_count, capacity, D), rows_dx.reshape(slot_count, capacity, D)],
        axis=1,
    )
    down_ready = after(grad_down.reshape(members, FF // members, D), part_up, back)
    rows_down = exchange(down_ready, "dev")
    back = exchange(after(back, rows_down), everyone).reshape(pair_rows, D)

    part_down = expert_sums(group_expert, rows_down)
    sum_up = lax.psum_scatter(part_up, "grp", scatter_dimension=0, tiled=True)
    sum_down = lax.psum_scatter(part_down, "grp", scatter_dimension=0, tiled=True)

    take_0 = row_x[0][:, None] == places[None, :]
    take_1 = row_x[1][:, None] == places[None, :]
    take_dx = (row_dy[0][:, None] == places[None, :]) | (row_dy[1][:, None] == places[None, :])
    taker = jnp.concatenate([take_0, take_1, take_dx], axis=0).astype(jnp.bfloat16)
    taken = jnp.dot(taker, back, preferred_element_type=jnp.float32)
    out_0 = taken[:tok_count]
    out_1 = taken[tok_count : 2 * tok_count]
    mixed = (route_weight[:, 0:1] * out_0 + route_weight[:, 1:2] * out_1).astype(jnp.bfloat16)
    token_grad = taken[2 * tok_count :].astype(jnp.bfloat16)
    mix_grad = jnp.stack(
        [jnp.sum(cot_float * out_0, axis=1), jnp.sum(cot_float * out_1, axis=1)], axis=1
    )

    trained_in, mean_in, square_in = adam_step(
        proj_in, first_in, second_in, sum_up.astype(jnp.float32)
    )
    trained_out, mean_out, square_out = adam_step(
        proj_out, first_out, second_out, sum_down.astype(jnp.float32)
    )
    return (
        mixed,
        token_grad,
        mix_grad,
        trained_in,
        mean_in,
        square_in,
        trained_out,
        mean_out,
        square_out,
    )


def solution(mesh):
    in_specs = (
        P(("grp", "dev"), None),
        P(("grp", "dev"), None),
        P(("grp", "dev"), None),
        P(),
        P(("grp", "dev"), None),
        P("grp", "dev", None),
        P("grp", "dev", None),
        P("grp", "dev", None),
        P("grp", "dev", None),
        P("grp", "dev", None),
        P("grp", "dev", None),
    )
    out_specs = (
        P(("grp", "dev"), None),
        P(("grp", "dev"), None),
        P(("grp", "dev"), None),
        P("grp", "dev", None),
        P("grp", "dev", None),
        P("grp", "dev", None),
        P("grp", "dev", None),
        P("grp", "dev", None),
        P("grp", "dev", None),
    )
    return jax.shard_map(
        on_device, mesh=mesh, in_specs=in_specs, out_specs=out_specs, check_vma=False
    )
```

```python
import jax
import jax.numpy as jnp
from jax import lax
from jax.experimental import pallas as pl
from jax.experimental.pallas import tpu as pltpu
from jax.sharding import PartitionSpec as P

D = 2048
FF = 1024
E = 16


beta_first = 0.9
beta_second = 0.95
learn_rate = 0.01
decay_rate = 0.1
adam_eps = 1e-08
bias_first = 1.0 - 0.9**10
bias_second = 1.0 - 0.95**10


def silu_parts(values):
    logistic = jax.nn.sigmoid(values)
    return (values * logistic, logistic * (1.0 + values * (1.0 - logistic)))


def adam_step(weight, moment, square, gradient):
    new_moment = beta_first * moment + (1.0 - beta_first) * gradient
    new_square = beta_second * square + (1.0 - beta_second) * gradient * gradient
    update = (
        new_moment / bias_first / (jnp.sqrt(new_square / bias_second) + adam_eps)
        + decay_rate * weight
    )
    return (weight - learn_rate * update, new_moment, new_square)


def after(value, *earlier):
    return lax.optimization_barrier((value,) + earlier)[0]


def expert_sums(experts, rows):
    members, depth, width = rows.shape
    tile = 16

    def kernel(expert_ref, rows_ref, out_ref, acc_ref):
        acc_ref[...] = jnp.zeros_like(acc_ref)

        def add(d, carry):
            e = expert_ref[d]
            acc_ref[e] = acc_ref[e] + rows_ref[d].astype(jnp.float32)
            return carry

        lax.fori_loop(0, members, add, 0)
        out_ref[...] = acc_ref[...].astype(out_ref.dtype)

    return pl.pallas_call(
        kernel,
        grid_spec=pltpu.PrefetchScalarGridSpec(
            num_scalar_prefetch=1,
            grid=(depth // tile,),
            in_specs=[pl.BlockSpec((members, tile, width), lambda i, e: (0, i, 0))],
            out_specs=pl.BlockSpec((E, tile, width), lambda i, e: (0, i, 0)),
            scratch_shapes=[pltpu.VMEM((E, tile, width), jnp.float32)],
        ),
        out_shape=jax.ShapeDtypeStruct((E, depth, width), jnp.bfloat16),
        compiler_params=pltpu.CompilerParams(vmem_limit_bytes=24 * 1024 * 1024),
        cost_estimate=pl.CostEstimate(
            flops=members * depth * width,
            bytes_accessed=2 * (members + E) * depth * width,
            transcendentals=0,
        ),
    )(experts, rows)


def pick_experts(stack, experts):
    return jnp.take(stack, experts, axis=0, mode="clip")


def exchange(payload, axes):
    return lax.all_to_all(payload, axes, split_axis=0, concat_axis=0, tiled=True)


def on_device(
    tokens,
    cotangent,
    route_weight,
    slot_expert,
    targets,
    proj_in,
    first_in,
    second_in,
    proj_out,
    first_out,
    second_out,
):
    groups = lax.axis_size("grp")
    members = lax.axis_size("dev")
    slot_count = groups * members
    everyone = ("grp", "dev")
    tok_count = tokens.shape[0]
    capacity = 3 * tok_count // slot_count
    pair = 2 * capacity
    pair_rows = slot_count * pair

    my_group = lax.axis_index("grp")
    group_expert = lax.dynamic_slice_in_dim(slot_expert, my_group * members, members)
    group_expert = jnp.clip(group_expert, 0, E - 1)
    low_out = proj_out.astype(jnp.bfloat16)
    all_down = lax.all_gather(low_out, "grp", axis=0, tiled=True)
    low_in = proj_in.astype(jnp.bfloat16)
    half = low_in.shape[1] // 2
    all_1 = lax.all_gather(low_in[:, :half], "grp", axis=0, tiled=True)
    all_2 = lax.all_gather(low_in[:, half:], "grp", axis=0, tiled=True)

    flat_target = targets.reshape(-1)
    onehot = (flat_target[:, None] == jnp.arange(slot_count, dtype=jnp.int32)[None, :]).astype(
        jnp.int32
    )
    earlier = jnp.cumsum(onehot, axis=0) - onehot
    position = jnp.sum(earlier * onehot, axis=1)
    within = position < capacity
    row = jnp.where(within, flat_target * pair + position, -pair_rows).reshape(tok_count, 2)
    row_x = [row[:, 0], row[:, 1]]
    row_dy = [row[:, 0] + capacity, row[:, 1] + capacity]
    places = jnp.arange(pair_rows, dtype=jnp.int32)

    hit_x = (places[:, None] == row_x[0][None, :]) | (places[:, None] == row_x[1][None, :])
    hit_0 = places[:, None] == row_dy[0][None, :]
    hit_1 = places[:, None] == row_dy[1][None, :]
    picker = jnp.concatenate([hit_x, hit_0, hit_1], axis=1).astype(jnp.bfloat16)
    cot_float = cotangent.astype(jnp.float32)
    scaled = [(route_weight[:, k : k + 1] * cot_float).astype(jnp.bfloat16) for k in (0, 1)]
    source = jnp.concatenate([tokens] + scaled, axis=0)
    send = jnp.dot(picker, source, preferred_element_type=jnp.float32).astype(jnp.bfloat16)
    slot_both = exchange(send.reshape(slot_count, pair, D), everyone)

    got_down = exchange(after(pick_experts(all_down, group_expert), slot_both), "dev")
    got_1 = exchange(after(pick_experts(all_1, group_expert), got_down), "dev")
    got_2 = exchange(after(pick_experts(all_2, group_expert), got_1), "dev")
    slot_rows = slot_count * capacity
    slot_x = slot_both[:, :capacity].reshape(slot_rows, D)
    slot_dy = slot_both[:, capacity:].reshape(slot_rows, D)
    split_x = slot_x.reshape(slot_rows, members, 2, half)
    x_1 = split_x[:, :, 0].reshape(slot_rows, members * half)
    x_2 = split_x[:, :, 1].reshape(slot_rows, members * half)
    up_1 = got_1.reshape(members * half, 2 * FF)
    up_2 = got_2.reshape(members * half, 2 * FF)
    slot_down = got_down.reshape(FF, D)

    across = (((1,), (1,)), ((), ()))
    down = (((0,), (0,)), ((), ()))
    dhidden = lax.dot_general(slot_dy, slot_down, across, preferred_element_type=jnp.float32)
    gate_up = jnp.dot(x_1, up_1, preferred_element_type=jnp.float32) + jnp.dot(
        x_2, up_2, preferred_element_type=jnp.float32
    )
    gating = gate_up[:, :FF]
    upward = gate_up[:, FF:]
    active, derivative = silu_parts(gating)
    hidden = (active * upward).astype(jnp.bfloat16)
    grad_gateup = jnp.concatenate([dhidden * upward * derivative, dhidden * active], axis=1).astype(
        jnp.bfloat16
    )

    def low_dot(a, b, dims):
        return lax.dot_general(a, b, dims, preferred_element_type=jnp.float32).astype(jnp.bfloat16)

    grad_1 = low_dot(x_1, grad_gateup, down).reshape(members, half, 2 * FF)
    rows_1 = exchange(grad_1, "dev")
    grad_2 = low_dot(x_2, grad_gateup, down).reshape(members, half, 2 * FF)
    grad_down = low_dot(hidden, slot_dy, down).reshape(members, FF // members, D)
    result = low_dot(hidden, slot_down, (((1,), (0,)), ((), ())))
    dx_1 = low_dot(grad_gateup, up_1, across)
    dx_2 = low_dot(grad_gateup, up_2, across)
    rows_dx = jnp.stack(
        [dx_1.reshape(slot_rows, members, half), dx_2.reshape(slot_rows, members, half)],
        axis=2,
    ).reshape(slot_rows, D)
    back = jnp.concatenate(
        [
            result.reshape(slot_count, capacity, D),
            rows_dx.reshape(slot_count, capacity, D),
        ],
        axis=1,
    )
    rows_2 = exchange(after(grad_2, rows_1), "dev")
    rows_down = exchange(after(grad_down, rows_2, back), "dev")
    back = exchange(after(back, rows_down), everyone).reshape(pair_rows, D)
    part_1 = expert_sums(group_expert, rows_1)
    part_2 = expert_sums(group_expert, rows_2)
    part_down = expert_sums(group_expert, rows_down)
    sum_1 = lax.psum_scatter(part_1, "grp", scatter_dimension=0, tiled=True)
    sum_2 = lax.psum_scatter(part_2, "grp", scatter_dimension=0, tiled=True)
    sum_down = lax.psum_scatter(part_down, "grp", scatter_dimension=0, tiled=True)
    sum_up = jnp.concatenate([sum_1, sum_2], axis=1)

    take_0 = row_x[0][:, None] == places[None, :]
    take_1 = row_x[1][:, None] == places[None, :]
    take_dx = (row_dy[0][:, None] == places[None, :]) | (row_dy[1][:, None] == places[None, :])
    taker = jnp.concatenate([take_0, take_1, take_dx], axis=0).astype(jnp.bfloat16)
    taken = jnp.dot(taker, back, preferred_element_type=jnp.float32)
    out_0 = taken[:tok_count]
    out_1 = taken[tok_count : 2 * tok_count]
    mixed = (route_weight[:, 0:1] * out_0 + route_weight[:, 1:2] * out_1).astype(jnp.bfloat16)
    token_grad = taken[2 * tok_count :].astype(jnp.bfloat16)
    mix_grad = jnp.stack(
        [jnp.sum(cot_float * out_0, axis=1), jnp.sum(cot_float * out_1, axis=1)], axis=1
    )

    trained_in, mean_in, square_in = adam_step(
        proj_in, first_in, second_in, sum_up.astype(jnp.float32)
    )
    trained_out, mean_out, square_out = adam_step(
        proj_out, first_out, second_out, sum_down.astype(jnp.float32)
    )
    return (
        mixed,
        token_grad,
        mix_grad,
        trained_in,
        mean_in,
        square_in,
        trained_out,
        mean_out,
        square_out,
    )


def solution(mesh):
    in_specs = (
        P(("grp", "dev"), None),
        P(("grp", "dev"), None),
        P(("grp", "dev"), None),
        P(),
        P(("grp", "dev"), None),
        P("grp", "dev", None),
        P("grp", "dev", None),
        P("grp", "dev", None),
        P("grp", "dev", None),
        P("grp", "dev", None),
        P("grp", "dev", None),
    )
    out_specs = (
        P(("grp", "dev"), None),
        P(("grp", "dev"), None),
        P(("grp", "dev"), None),
        P("grp", "dev", None),
        P("grp", "dev", None),
        P("grp", "dev", None),
        P("grp", "dev", None),
        P("grp", "dev", None),
        P("grp", "dev", None),
    )
    return jax.shard_map(
        on_device, mesh=mesh, in_specs=in_specs, out_specs=out_specs, check_vma=False
    )
```
